32 devices in a mesh: ctx: 4 (over z), head: 2 (over y), dp: 4 (over x, core).
Axes of the slice: x: 2, y: 2, z: 4, core: 2. Of those that a mesh axis runs over, the one named last changes fastest.
Arguments:
- queries: bfloat16 [4, 2048, 1024], P('dp', 'ctx', 'head'), may hold values from -4.5 to 4.5
- key_vectors: bfloat16 [4, 2048, 1024], P('dp', 'ctx', 'head'), may hold values from -4.5 to 4.5
- value_vectors: bfloat16 [4, 2048, 1024], P('dp', 'ctx', 'head'), may hold values from -18 to 18
- cotangent: bfloat16 [4, 2048, 2048], P('dp', 'ctx', 'head'), may hold values from -6 to 6
- w_out: bfloat16 [1024, 2048], P('head'), may hold values from -0.1875 to 0.1875
- phoneme_keys: bfloat16 [4, 256, 1024], P('dp', None, 'head'), may hold values from -5 to 5
- phoneme_values: bfloat16 [4, 256, 1024], P('dp', None, 'head'), may hold values from -18 to 18
- phrase_blocks: int32 [4, 16, 4], P('dp'), may hold values from 0 to 15, as said below
- phrase_count: int32 [4, 16], P('dp', 'ctx'), may hold values from 0 to 4, as said below
- alignment: int32 [4, 2048], P('dp', 'ctx'), may hold values from 0 to 255, as said below
Outputs:
- layer_out: bfloat16 [4, 2048, 2048], P('dp', 'ctx', 'head')
- d_queries: bfloat16 [4, 2048, 1024], P('dp', 'ctx', 'head')
- d_keys: bfloat16 [4, 2048, 1024], P('dp', 'ctx', 'head')
- d_values: bfloat16 [4, 2048, 1024], P('dp', 'ctx', 'head')
- d_phoneme_keys: bfloat16 [4, 256, 1024], P('dp', None, 'head')
- d_phoneme_values: bfloat16 [4, 256, 1024], P('dp', None, 'head')
- d_w_out: float32 [1024, 2048], P('head', ('ctx', 'dp'))
The draws below stay inside these ranges and needn't reach their ends.
Inputs may be any that keep to these rules, and one draw needn't show every extreme that they name: `phrase_blocks`: block j lies on index j // 4 of ctx. Every entry names a block on another index than its query block; all entries of the query blocks of one index that lie on the same other index name the same block; no entry names the first block of the next index or the last block of the previous index. `phrase_count`: the first query block of every index of ctx has all 4 slots in use. alignment[b, t] lies within 2 of t * 256 // 2048; the first frame is aligned to phoneme 0 and the last to phoneme 256 - 1.
All inputs are finite; a program needn't handle non-finite values.
Results may differ from the reference program's by a relative error of at most 0.018.
Values may be sent and summed in bfloat16 or wider, within the bound.
No kernel may reach another device: no remote copies, remote signals or barrier semaphores. Data moves between devices by JAX's collectives and lax.ppermute only.
A program may use at most 128 MiB of HBM per device.

```python
import math
import jax
import jax.numpy as jnp
from jax import lax

D = 2048
DH = 128
BLK = 128
HALF_BAND = 64
PHRASE_SLOTS = 4
PH_HALF = 16
F_DEV = 512
PH = 256
HD = 1024
SEQ = 2048
NBLK = 16
BATCH = 4
N_CTX = 4


def draw_queries(key, part):
    own_key = jax.random.fold_in(key, 1)
    result = jnp.clip(jax.random.normal(own_key, (BATCH, SEQ, HD)), -4.5, 4.5)
    return result.astype(jnp.bfloat16)


def draw_key_vectors(key, part):
    own_key = jax.random.fold_in(key, 2)
    result = jnp.clip(jax.random.normal(own_key, (BATCH, SEQ, HD)), -4.5, 4.5)
    return result.astype(jnp.bfloat16)


def draw_phrase_blocks(key, part):
    per_dev = F_DEV // BLK
    ctx_count = NBLK // per_dev
    first_key, second_key, third_key, fourth_key = jax.random.split(key, 4)
    draw_shape = (BATCH, ctx_count, ctx_count)
    any_block = jax.random.randint(first_key, draw_shape, 0, per_dev)
    after_first = jax.random.randint(second_key, draw_shape, 1, per_dev)
    before_last = jax.random.randint(third_key, draw_shape, 0, per_dev - 1)
    destination = jnp.arange(ctx_count)[:, None]
    source = jnp.arange(ctx_count)[None, :]
    pool = jnp.where(source == destination + 1, after_first, jnp.where(source == destination - 1, before_last, any_block))
    owner_dev = jnp.arange(NBLK) // per_dev
    offset = jax.random.randint(fourth_key, (BATCH, NBLK, PHRASE_SLOTS), 1, ctx_count)
    source_dev = (owner_dev[None, :, None] + offset) % ctx_count
    pool_rows = pool[:, owner_dev, :]
    chosen = jnp.take_along_axis(pool_rows, source_dev, axis=2)
    return (source_dev * per_dev + chosen).astype(jnp.int32)


def draw_phrase_count(key, part):
    per_dev = F_DEV // BLK
    counts = jax.random.randint(key, (BATCH, NBLK), 0, PHRASE_SLOTS + 1)
    first_frame_on_device = (jnp.arange(NBLK) % per_dev == 0)[None, :]
    return jnp.where(first_frame_on_device, PHRASE_SLOTS, counts).astype(jnp.int32)


def draw_alignment(key, part):
    frame_ids = jnp.arange(SEQ)
    base_value = frame_ids * PH // SEQ
    jitter = jax.random.randint(key, (BATCH, SEQ), -2, 3)
    result = jnp.clip(base_value[None, :] + jitter, 0, PH - 1)
    result = jnp.where(frame_ids[None, :] == 0, 0, result)
    result = jnp.where(frame_ids[None, :] == SEQ - 1, PH - 1, result)
    return result.astype(jnp.int32)


def strengthened(values, key, source, target, blocks, factor):
    owner, partner = [(jnp.arange(values.shape[dim]) // (values.shape[dim] // blocks)).reshape([-1 if axis == dim else 1 for axis in range(values.ndim)]) for dim in (source, target)]
    chosen = jax.random.permutation(key, blocks)[partner]
    strong = (owner == chosen) | (owner == (partner + blocks // 2) % blocks)
    return jnp.where(strong, factor * values, values)


def levels(key, dims, cuts, smallest, largest):
    loudness = 1.0
    for axis_at, blocks in cuts:
        steps = jax.random.uniform(jax.random.fold_in(jax.random.fold_in(key, 6), axis_at), (blocks,), jnp.float32, smallest / len(cuts), largest / len(cuts))
        loudness = loudness * jnp.repeat(jnp.exp(steps), dims[axis_at] // blocks).reshape((-1,) + (1,) * (len(dims) - 1 - axis_at))
    return loudness


def gaussian(key, shape, scale, limit, cuts=(), kind=jnp.bfloat16):
    loudness = levels(key, shape, cuts, -0.22, 0.18) if cuts else 1.0
    values = jax.random.normal(key, shape, jnp.float32) * scale * loudness
    return jnp.minimum(jnp.maximum(values, -limit), limit).astype(kind)


def heavy_noise(key, dims, scale, limit, pieces, heavy, held_as=jnp.bfloat16):
    values = scale * jax.random.normal(key, dims, jnp.float32)
    if pieces:
        values = values * levels(key, dims, pieces, -0.22, 0.18)
    return jnp.clip(strengthened(values, jax.random.fold_in(key, 3), *heavy), -limit, limit).astype(held_as)


def setup_inputs(seed: int = 0) -> dict:
    streams_of = jax.random.split(jax.random.key(seed), 11)
    queries = draw_queries(jax.random.fold_in(streams_of[10], 71), 0)
    key_vectors = draw_key_vectors(jax.random.fold_in(streams_of[10], 71), 0)
    value_vectors = gaussian(streams_of[2], (BATCH, SEQ, HD), 3.0, 18.0, ((0, 4), (1, 4), (2, 2)))
    cotangent = heavy_noise(streams_of[3], (BATCH, SEQ, D), 1.0, 6.0, ((0, 4), (1, 4), (2, 2)), (1, 2, 4, 2.0))
    w_out = gaussian(streams_of[4], (HD, D), HD ** -0.5, 0.1875, ((0, 2),))
    phoneme_keys = gaussian(streams_of[5], (BATCH, PH, HD), 1.0, 5.0, ((0, 4), (2, 2)))
    phoneme_values = gaussian(streams_of[6], (BATCH, PH, HD), 3.0, 18.0, ((0, 4), (2, 2)))
    phrase_blocks = draw_phrase_blocks(jax.random.fold_in(streams_of[10], 71), 0)
    phrase_count = draw_phrase_count(jax.random.fold_in(streams_of[10], 71), 0)
    alignment = draw_alignment(jax.random.fold_in(streams_of[10], 71), 0)
    return {"queries": queries, "key_vectors": key_vectors, "value_vectors": value_vectors, "cotangent": cotangent, "w_out": w_out, "phoneme_keys": phoneme_keys, "phoneme_values": phoneme_values, "phrase_blocks": phrase_blocks, "phrase_count": phrase_count, "alignment": alignment}


masked_score = -1e+30

def round_half(values_in):
    return lax.optimization_barrier(values_in.astype(jnp.bfloat16))

def attend(query_rows, kv_pad, kv_phrase, phone_keys, phone_values, grad_out, first_frame, slot_count, aligned, seq_len):
    frames, feat_width = query_rows.shape
    block_count = frames // BLK
    head_count = feat_width // DH
    score_scale = DH ** (-0.5)

    def product(form, left, right):
        return jnp.einsum(form, left.astype(jnp.float32), right.astype(jnp.float32), preferred_element_type=jnp.float32, precision=lax.Precision.HIGHEST)
    padded = kv_pad.reshape(block_count + 2, BLK, 2 * feat_width)
    band_rows = jnp.concatenate([padded[0:block_count], padded[1:block_count + 1], padded[2:block_count + 2]], axis=1)
    phrase_rows = kv_phrase.reshape(block_count, PHRASE_SLOTS * BLK, 2 * feat_width)
    phone_pair = jnp.concatenate([phone_keys, phone_values], axis=1)
    phone_rows = jnp.broadcast_to(phone_pair[None], (block_count, PH, 2 * feat_width))
    all_rows = jnp.concatenate([band_rows, phrase_rows, phone_rows], axis=1)
    key_count = all_rows.shape[1]
    key_heads = all_rows[:, :, :feat_width].reshape(block_count, key_count, head_count, DH)
    value_heads = all_rows[:, :, feat_width:].reshape(block_count, key_count, head_count, DH)
    row_index = jnp.arange(BLK).astype(jnp.int32)
    block_index = jnp.arange(block_count).astype(jnp.int32)
    query_pos = first_frame + block_index[:, None] * BLK + row_index[None, :]
    band_cols = jnp.arange(3 * BLK).astype(jnp.int32)
    key_pos = first_frame - BLK + block_index[:, None] * BLK + band_cols[None, :]
    distance = query_pos[:, :, None] - key_pos[:, None, :]
    band_ok = (jnp.abs(distance) <= HALF_BAND) & (key_pos[:, None, :] >= 0) & (key_pos[:, None, :] < seq_len)
    slot_index = jnp.arange(PHRASE_SLOTS * BLK).astype(jnp.int32) // BLK
    phrase_ok = jnp.broadcast_to((slot_index[None, :] < slot_count[:, None])[:, None, :], (block_count, BLK, PHRASE_SLOTS * BLK))
    phone_index = jnp.arange(PH).astype(jnp.int32)
    phone_ok = jnp.abs(phone_index[None, None, :] - aligned.reshape(block_count, BLK)[:, :, None]) <= PH_HALF
    key_mask = jnp.concatenate([band_ok, phrase_ok, phone_ok], axis=2)
    query_heads = query_rows.reshape(block_count, BLK, head_count, DH)
    scores = product('irhd,ikhd->ihrk', query_heads, key_heads) * score_scale
    scores = jnp.where(key_mask[:, None], scores, masked_score)
    row_max = lax.optimization_barrier(jnp.max(scores, axis=-1, keepdims=True))
    exp_scores = jnp.exp(scores - row_max)
    prob32 = exp_scores / lax.optimization_barrier(jnp.sum(exp_scores, axis=-1, keepdims=True))
    weights_half = round_half(prob32)
    attended = round_half(product('ihrk,ikhd->irhd', weights_half, value_heads))
    grad_heads = grad_out.reshape(block_count, BLK, head_count, DH)
    delta_row = lax.optimization_barrier(jnp.sum(grad_heads.astype(jnp.float32) * attended.astype(jnp.float32), axis=-1))
    delta_row = jnp.transpose(delta_row, (0, 2, 1))[..., None]
    d_weights = product('irhd,ikhd->ihrk', grad_heads, value_heads)
    d_scores = round_half(prob32 * (d_weights - delta_row) * score_scale)
    d_query = product('ihrk,ikhd->irhd', d_scores, key_heads).reshape(frames, feat_width)
    d_key_rows = product('ihrk,irhd->ikhd', d_scores, query_heads).reshape(block_count, key_count, feat_width)
    d_value_rows = product('ihrk,irhd->ikhd', weights_half, grad_heads).reshape(block_count, key_count, feat_width)
    d_both = jnp.concatenate([d_key_rows, d_value_rows], axis=-1)
    band_grads = d_both[:, :3 * BLK].reshape(block_count, 3, BLK, 2 * feat_width)
    pad_sum = jnp.pad(band_grads[:, 0], ((0, 2), (0, 0), (0, 0))) + jnp.pad(band_grads[:, 1], ((1, 1), (0, 0), (0, 0))) + jnp.pad(band_grads[:, 2], ((2, 0), (0, 0), (0, 0)))
    phrase_grads = d_both[:, 3 * BLK:3 * BLK + PHRASE_SLOTS * BLK].reshape(block_count, PHRASE_SLOTS, BLK, 2 * feat_width)
    phone_grads = lax.optimization_barrier(jnp.sum(d_both[:, 3 * BLK + PHRASE_SLOTS * BLK:], axis=0))
    return (attended.reshape(frames, feat_width), d_query, pad_sum, phrase_grads, phone_grads)

def reference(queries, key_vectors, value_vectors, cotangent, w_out, phoneme_keys, phoneme_values, phrase_blocks, phrase_count, alignment):
    per_dev = F_DEV // BLK
    outputs = []
    d_query_list = []
    d_key_list = []
    d_value_list = []
    d_phone_keys = []
    d_phone_values = []
    weight_sum = jnp.zeros((HD, D), jnp.float32)
    for batch_index in range(BATCH):
        query_all = queries[batch_index]
        key_value_gathered = jnp.concatenate([key_vectors[batch_index], value_vectors[batch_index]], axis=1)
        zero_rim = jnp.zeros((BLK, 2 * HD), key_value_gathered.dtype)
        kv_padded = jnp.concatenate([zero_rim, key_value_gathered, zero_rim], axis=0)
        kv_blocks = key_value_gathered.reshape(NBLK, BLK, 2 * HD)
        grad_all = jnp.dot(cotangent[batch_index], w_out.T, preferred_element_type=jnp.float32).astype(jnp.bfloat16)
        block_table = phrase_blocks[batch_index]
        counts_all = phrase_count[batch_index]
        align_all = alignment[batch_index]
        phone_k = phoneme_keys[batch_index]
        phoneme_value_rows = phoneme_values[batch_index]

        def device_step(loop_index, state_tuple):
            attended_all, d_query_all, grads_total, phone_total = state_tuple
            device = jnp.asarray(loop_index).astype(jnp.int32)
            first_frame = device * F_DEV
            first_block = device * per_dev
            query_rows = lax.dynamic_slice_in_dim(query_all, first_frame, F_DEV, 0)
            kv_pad = lax.dynamic_slice_in_dim(kv_padded, first_frame, F_DEV + 2 * BLK, 0)
            own_refs = lax.dynamic_slice_in_dim(block_table, first_block, per_dev, 0)
            kv_phrase = kv_blocks[own_refs]
            slot_count = lax.dynamic_slice_in_dim(counts_all, first_block, per_dev, 0)
            aligned = lax.dynamic_slice_in_dim(align_all, first_frame, F_DEV, 0)
            grad_rows = lax.dynamic_slice_in_dim(grad_all, first_frame, F_DEV, 0)
            attended, d_query, pad_sum, phrase_grads, phone_grads = attend(query_rows, kv_pad, kv_phrase, phone_k, phoneme_value_rows, grad_rows, first_frame, slot_count, aligned, SEQ)
            low_edge = round_half(pad_sum[0:1]).astype(jnp.float32)
            high_edge = round_half(pad_sum[per_dev + 1:]).astype(jnp.float32)
            slab = jnp.concatenate([low_edge, pad_sum[1:per_dev + 1], high_edge], axis=0)
            current = lax.dynamic_slice_in_dim(grads_total, first_block, per_dev + 2, 0)
            grads_total = lax.dynamic_update_slice_in_dim(grads_total, current + slab, first_block, 0)
            sources = (own_refs // per_dev).reshape(-1)
            local_block = (own_refs % per_dev).reshape(-1)
            device_ids = jnp.arange(N_CTX).astype(jnp.int32)
            onehot = sources[:, None] == device_ids[None, :]
            slot_sum = jnp.einsum('js,jrf->srf', onehot.astype(jnp.float32), phrase_grads.reshape(-1, BLK, 2 * HD), precision=lax.Precision.HIGHEST)
            chosen = lax.optimization_barrier(jnp.max(jnp.where(onehot, local_block[:, None], 0), axis=0))
            targets = device_ids * per_dev + chosen + 1
            grads_total = grads_total.at[targets].add(round_half(slot_sum).astype(jnp.float32))
            attended_all = lax.dynamic_update_slice_in_dim(attended_all, attended, first_frame, 0)
            d_query_all = lax.dynamic_update_slice_in_dim(d_query_all, d_query.astype(jnp.bfloat16), first_frame, 0)
            phone_total = phone_total + phone_grads
            return (attended_all, d_query_all, grads_total, phone_total)
        init_state = (jnp.zeros((SEQ, HD), queries.dtype), jnp.zeros((SEQ, HD), queries.dtype), jnp.zeros((NBLK + 2, BLK, 2 * HD), jnp.float32), jnp.zeros((PH, 2 * HD), jnp.float32))
        attended_all, d_query_all, grads_total, phone_total = lax.fori_loop(0, N_CTX, device_step, init_state)
        d_both = grads_total[1:NBLK + 1].reshape(SEQ, 2 * HD).astype(jnp.bfloat16)
        phone_half = phone_total.astype(jnp.bfloat16)
        outputs.append(jnp.dot(attended_all, w_out, preferred_element_type=jnp.float32).astype(jnp.bfloat16))
        d_query_list.append(d_query_all)
        d_key_list.append(d_both[:, :HD])
        d_value_list.append(d_both[:, HD:])
        d_phone_keys.append(phone_half[:, :HD])
        d_phone_values.append(phone_half[:, HD:])
        weight_sum = weight_sum + jnp.dot(attended_all.T, cotangent[batch_index], preferred_element_type=jnp.float32)
    d_w_out = weight_sum * (1.0 / math.sqrt(BATCH * SEQ))
    return (jnp.stack(outputs), jnp.stack(d_query_list), jnp.stack(d_key_list), jnp.stack(d_value_list), jnp.stack(d_phone_keys), jnp.stack(d_phone_values), d_w_out)
```

```python
import functools
import math

import jax
import jax.numpy as jnp
from jax import lax
from jax.experimental import pallas as pl
from jax.experimental.pallas import tpu as pltpu
from jax.sharding import PartitionSpec as P

DH = 128
BLK = 128
HALF_BAND = 64
PHRASE_SLOTS = 4
PH_HALF = 16
PH_PAD = 32
CHUNKS = 1
NEG = -1e30
LOG2E = math.log2(math.e)

F32 = jnp.float32
BF16 = jnp.bfloat16
SMEM = pltpu.SMEM
VMEM = pltpu.VMEM


def mm(left, right, dims):
    return lax.dot_general(left, right, (dims, ((), ())), preferred_element_type=F32)


NT = ((1,), (1,))
NN = ((1,), (0,))
TN = ((0,), (0,))


def spec(space=VMEM):
    return pl.BlockSpec(memory_space=space)


def rotated(value, axis, by):
    count = lax.axis_size(axis)
    return lax.ppermute(value, axis, [(i, (i + by) % count) for i in range(count)])


def shifted(value, axis, by):
    count = lax.axis_size(axis)
    pairs = [(i, i + by) for i in range(count) if 0 <= i + by < count]
    return lax.ppermute(value, axis, pairs)


def swapped(value, axis, bit):
    count = lax.axis_size(axis)
    return lax.ppermute(value, axis, [(i, i ^ bit) for i in range(count)])


def prepare_kernel(n, groups, fixed, chunks, table, counts, key, value, *outs):
    frames, width = key.shape
    blocks = frames // BLK
    part = width // chunks
    me = lax.axis_index("ctx")
    low = outs[0]
    high = outs[1]
    sends = outs[2 : 2 + chunks * (n - 1)]
    chosen, place, bias = outs[2 + chunks * (n - 1) :]
    low[0] = key[0:HALF_BAND, :]
    low[1] = value[0:HALF_BAND, :]
    high[0] = key[frames - HALF_BAND : frames, :]
    high[1] = value[frames - HALF_BAND : frames, :]
    for d in range(1, n):
        target = lax.rem(me + d, n)
        best = jnp.int32(0)
        for i in range(blocks):
            for p in range(PHRASE_SLOTS):
                entry = table[0, target * blocks + i, p]
                best = jnp.where(entry // blocks == me, entry % blocks, best)
        chosen[d - 1] = best
        rows = pl.ds(pl.multiple_of(best * BLK, BLK), BLK)
        for c in range(chunks):
            cols = slice(c * part, (c + 1) * part)
            out = sends[c * (n - 1) + d - 1]
            out[0] = key[rows, cols]
            out[1] = value[rows, cols]
    log2s = [math.log2(max(m, 1)) for m in range(PHRASE_SLOTS + 1)]
    for i in range(blocks):
        names = [table[0, me * blocks + i, p] // blocks for p in range(PHRASE_SLOTS)]
        hops = [lax.rem(me - name + n, n) - 1 for name in names]
        for g in range(groups):
            if fixed:
                times = jnp.int32(0)
                for p in range(PHRASE_SLOTS):
                    hit = (hops[p] == g) & (p < counts[0, i])
                    times = times + jnp.where(hit, 1, 0)
                place[i, g] = jnp.int32(g)
            else:
                times = jnp.where(g < counts[0, i], 1, 0)
                place[i, g] = hops[g]
            term = jnp.float32(NEG)
            for m in range(1, PHRASE_SLOTS + 1):
                term = jnp.where(times == m, jnp.float32(log2s[m]), term)
            bias[i, g] = term


def prepare(n, groups, fixed, table, counts, key, value):
    frames, width = key.shape
    blocks = frames // BLK
    halo = jax.ShapeDtypeStruct((2, HALF_BAND, width), BF16)
    block = jax.ShapeDtypeStruct((2, BLK, width // CHUNKS), BF16)
    count = CHUNKS * (n - 1)
    outs = pl.pallas_call(
        functools.partial(prepare_kernel, n, groups, fixed, CHUNKS),
        name="prepare",
        out_shape=[halo, halo]
        + [block] * count
        + [
            jax.ShapeDtypeStruct((n - 1,), jnp.int32),
            jax.ShapeDtypeStruct((blocks, groups), jnp.int32),
            jax.ShapeDtypeStruct((blocks, groups), F32),
        ],
        in_specs=[spec(SMEM), spec(SMEM), spec(), spec()],
        out_specs=[spec()] * (2 + count) + [spec(SMEM)] * 3,
    )(table, counts, key, value)
    sends = outs[2 : 2 + count]
    sends = [sends[c * (n - 1) : (c + 1) * (n - 1)] for c in range(CHUNKS)]
    return outs[0], outs[1], sends, outs[2 + count :]


def attend_kernel(n, groups, fixed, own_phones, phones, *refs):
    (place, bias, aligned, query, grad, key, value, low, high, phone_k, phone_v), refs = (
        refs[:11],
        refs[11:],
    )
    received, refs = refs[: n - 1], refs[n - 1 :]
    (attended, d_query, d_key, d_value, to_prev, to_next, phone_own), refs = refs[:7], refs[7:]
    returns, refs = refs[: n - 1], refs[n - 1 :]
    (kpad, vpad, kfix, vfix, zfix, pfix, pband, dsfix, dkpad, dvpad, acc, acc_phone), refs = (
        refs[:12],
        refs[12:],
    )
    frames = query.shape[0]
    blocks = frames // BLK
    window = phone_k.shape[0]
    phrase = groups * BLK
    me = lax.axis_index("ctx")
    scale = DH**-0.5
    to_log2 = scale * LOG2E
    band = 2 * HALF_BAND + BLK

    kpad[0:HALF_BAND] = low[0]
    kpad[HALF_BAND : HALF_BAND + frames] = key[...]
    kpad[HALF_BAND + frames :] = high[0]
    vpad[0:HALF_BAND] = low[1]
    vpad[HALF_BAND : HALF_BAND + frames] = value[...]
    vpad[HALF_BAND + frames :] = high[1]
    kfix[phrase:] = phone_k[...]
    vfix[phrase:] = phone_v[...]
    dkpad[...] = jnp.zeros_like(dkpad)
    dvpad[...] = jnp.zeros_like(dvpad)
    if fixed:
        for g in range(groups):
            kfix[g * BLK : (g + 1) * BLK] = received[g][0]
            vfix[g * BLK : (g + 1) * BLK] = received[g][1]
    else:
        (stack,) = refs
        for g in range(n - 1):
            stack[g] = received[g][...]
        acc[...] = jnp.zeros_like(acc)
        acc_phone[...] = jnp.zeros_like(acc_phone)

    row = lax.broadcasted_iota(jnp.int32, (BLK, band), 0)
    col = lax.broadcasted_iota(jnp.int32, (BLK, band), 1)
    ahead = col - row
    inside = (ahead >= 0) & (ahead <= 2 * HALF_BAND)
    phone = lax.broadcasted_iota(jnp.int32, (BLK, window), 1) + (me * own_phones - PH_PAD)
    real = (phone >= 0) & (phone < phones)

    size = frames if fixed else BLK
    for start in range(0, frames, size):
        rows = slice(start, start + size)
        if not fixed:
            for g in range(groups):
                there = place[start // BLK, g]
                kfix[g * BLK : (g + 1) * BLK] = stack[there, 0]
                vfix[g * BLK : (g + 1) * BLK] = stack[there, 1]
        zfix[...] = mm(query[rows], kfix[...], NT)
        for s in range(start, start + size, BLK):
            i = s // BLK
            here = slice(s - start, s - start + BLK)
            mask = inside
            if i == 0:
                mask = mask & ((col >= HALF_BAND) | (me > 0))
            if i == blocks - 1:
                mask = mask & ((col < band - HALF_BAND) | (me < n - 1))
            zb = mm(query[s : s + BLK], kpad[s : s + band], NT) * to_log2
            zb = jnp.where(mask, zb, NEG)
            pieces = []
            for g in range(groups):
                pieces.append(zfix[here, g * BLK : (g + 1) * BLK] * to_log2 + bias[i, g])
            near = jnp.abs(phone - aligned[s : s + BLK]) <= PH_HALF
            zp = jnp.where(near & real, zfix[here, phrase:] * to_log2, NEG)
            zf = jnp.concatenate(pieces + [zp], axis=1)
            top = jnp.maximum(
                jnp.max(zb, axis=1, keepdims=True), jnp.max(zf, axis=1, keepdims=True)
            )
            eb = jnp.exp2(zb - top)
            ef = jnp.exp2(zf - top)
            total = jnp.sum(eb, axis=1, keepdims=True) + jnp.sum(ef, axis=1, keepdims=True)
            inverse = 1.0 / total
            pband[here] = (eb * inverse).astype(BF16)
            pfix[here] = (ef * inverse).astype(BF16)
        out_fix = mm(pfix[...], vfix[...], NN)
        d_fix = mm(grad[rows], vfix[...], NT)
        for s in range(start, start + size, BLK):
            here = slice(s - start, s - start + BLK)
            there = slice(s, s + BLK)
            reach = slice(s, s + band)
            weights = pband[here]
            out = (mm(weights, vpad[reach], NN) + out_fix[here]).astype(BF16)
            attended[there] = out
            g_here = grad[there]
            q_here = query[there]
            delta = jnp.sum(out.astype(F32) * g_here.astype(F32), axis=1, keepdims=True)
            d_band = mm(g_here, vpad[reach], NT)
            ds = (weights.astype(F32) * (d_band - delta)).astype(BF16)
            dsfix[here] = (pfix[here].astype(F32) * (d_fix[here] - delta)).astype(BF16)
            dq = mm(ds, kpad[reach], NN) + mm(dsfix[here], kfix[...], NN)
            d_query[there] = (dq * scale).astype(BF16)
            dkpad[reach] += mm(ds, q_here, TN)
            dvpad[reach] += mm(weights, g_here, TN)
        dk = mm(dsfix[...], query[rows], TN) * scale
        dv = mm(pfix[...], grad[rows], TN)
        if fixed:
            for g in range(groups):
                returns[g][0] = dk[g * BLK : (g + 1) * BLK].astype(BF16)
                returns[g][1] = dv[g * BLK : (g + 1) * BLK].astype(BF16)
            acc_phone[0] = dk[phrase:]
            acc_phone[1] = dv[phrase:]
        else:
            for g in range(groups):
                there = place[start // BLK, g]
                acc[there, 0] += dk[g * BLK : (g + 1) * BLK]
                acc[there, 1] += dv[g * BLK : (g + 1) * BLK]
            acc_phone[0] += dk[phrase:]
            acc_phone[1] += dv[phrase:]
    if not fixed:
        for g in range(n - 1):
            returns[g][...] = acc[g].astype(BF16)
    d_key[...] = dkpad[HALF_BAND : HALF_BAND + frames] * scale
    d_value[...] = dvpad[HALF_BAND : HALF_BAND + frames]
    to_prev[0, 0:HALF_BAND] = (dkpad[0:HALF_BAND] * scale).astype(BF16)
    to_prev[1, 0:HALF_BAND] = dvpad[0:HALF_BAND].astype(BF16)
    to_next[0, 0:HALF_BAND] = (dkpad[HALF_BAND + frames :] * scale).astype(BF16)
    to_next[1, 0:HALF_BAND] = dvpad[HALF_BAND + frames :].astype(BF16)
    to_prev[:, HALF_BAND:] = acc_phone[:, 0:PH_PAD].astype(BF16)
    phone_own[...] = acc_phone[:, PH_PAD : PH_PAD + own_phones]
    above = PH_PAD + own_phones
    to_next[:, HALF_BAND:] = acc_phone[:, above : above + PH_PAD].astype(BF16)


def attend(
    n, groups, fixed, own_phones, phones, chunk, index, aligned, query, grad, key, value, halos, phone_kv, received
):
    place, bias = index
    frames, width = query.shape
    window = phone_kv[0].shape[0]
    part = width // CHUNKS
    heads = part // DH
    first = chunk * heads
    column = lambda rows: pl.BlockSpec((rows, DH), lambda h: (0, first + h))
    out_column = lambda rows: pl.BlockSpec((rows, DH), lambda h: (0, h))
    pair = lambda rows: pl.BlockSpec((2, rows, DH), lambda h: (0, 0, first + h))
    out_pair = lambda rows: pl.BlockSpec((2, rows, DH), lambda h: (0, 0, h))
    edge = HALF_BAND + PH_PAD
    fix = groups * BLK + window
    size = frames if fixed else BLK
    band = BLK + 2 * HALF_BAND
    shape = jax.ShapeDtypeStruct
    scratch = [
        VMEM((frames + 2 * HALF_BAND, DH), BF16),
        VMEM((frames + 2 * HALF_BAND, DH), BF16),
        VMEM((fix, DH), BF16),
        VMEM((fix, DH), BF16),
        VMEM((size, fix), F32),
        VMEM((size, fix), BF16),
        VMEM((size, band), BF16),
        VMEM((size, fix), BF16),
        VMEM((frames + 2 * HALF_BAND, DH), F32),
        VMEM((frames + 2 * HALF_BAND, DH), F32),
        VMEM((n - 1, 2, BLK, DH), F32),
        VMEM((2, window, DH), F32),
    ]
    if not fixed:
        scratch.append(VMEM((n - 1, 2, BLK, DH), BF16))
    keys = band + fix
    return pl.pallas_call(
        functools.partial(attend_kernel, n, groups, fixed, own_phones, phones),
        name="attend",
        grid=(heads,),
        out_shape=[
            shape((frames, part), BF16),
            shape((frames, part), BF16),
            shape((frames, part), F32),
            shape((frames, part), F32),
            shape((2, edge, part), BF16),
            shape((2, edge, part), BF16),
            shape((2, own_phones, part), F32),
        ]
        + [shape((2, BLK, part), BF16)] * (n - 1),
        in_specs=[spec(SMEM), spec(SMEM), pl.BlockSpec((frames, 1), lambda h: (0, 0))]
        + [column(frames)] * 4
        + [pair(HALF_BAND)] * 2
        + [column(window)] * 2
        + [out_pair(BLK)] * (n - 1),
        out_specs=[out_column(frames)] * 4
        + [out_pair(edge)] * 2
        + [out_pair(own_phones)]
        + [out_pair(BLK)] * (n - 1),
        scratch_shapes=scratch,
        cost_estimate=pl.CostEstimate(
            flops=12 * frames * keys * part,
            bytes_accessed=16 * frames * part,
            transcendentals=frames * keys * heads,
        ),
    )(place, bias, aligned, query, grad, key, value, *halos, *phone_kv, *received)


def weight_kernel(half, block, attended, own, other, out, turned):
    s = pl.program_id(0)

    @pl.when(s == 0)
    def _():
        turned[...] = attended[...].T

    @pl.when(half[s] == 0)
    def _():
        out[0] = mm(turned[...], own[...], NN).astype(BF16)

    @pl.when(half[s] != 0)
    def _():
        out[0] = mm(turned[...], other[...], NN).astype(BF16)


def weight_terms(half, block, attended, own, other, size):
    frames, width = attended.shape
    count = half.shape[0]
    column = pl.BlockSpec((frames, size), lambda s, half, block: (0, block[s]))
    return pl.pallas_call(
        weight_kernel,
        name="weight",
        grid_spec=pltpu.PrefetchScalarGridSpec(
            num_scalar_prefetch=2,
            grid=(count,),
            in_specs=[
                pl.BlockSpec((frames, width), lambda s, half, block: (0, 0)),
                column,
                column,
            ],
            out_specs=pl.BlockSpec((1, width, size), lambda s, half, block: (s, 0, 0)),
            scratch_shapes=[VMEM((width, frames), BF16)],
        ),
        out_shape=jax.ShapeDtypeStruct((count, width, size), BF16),
        cost_estimate=pl.CostEstimate(
            flops=2 * frames * width * count * size,
            bytes_accessed=4 * width * count * size,
            transcendentals=0,
        ),
    )(half, block, attended, own, other)


def finish_kernel(n, own_phones, chosen, own_k, own_v, low, high, *refs):
    returned, refs = refs[: n - 1], refs[n - 1 :]
    phones, refs = refs[:n], refs[n:]
    d_key, d_value, d_phone_k, d_phone_v, sum_k, sum_v = refs
    frames = own_k.shape[0]
    me = lax.axis_index("ctx")
    sum_k[...] = own_k[...]
    sum_v[...] = own_v[...]
    for side, total in enumerate((sum_k, sum_v)):
        total[0:HALF_BAND] += low[side, 0:HALF_BAND].astype(F32)
        total[frames - HALF_BAND : frames] += high[side, 0:HALF_BAND].astype(F32)
        for d in range(n - 1):
            rows = pl.ds(pl.multiple_of(chosen[d] * BLK, BLK), BLK)
            total[rows] += returned[d][side].astype(F32)
    d_key[...] = sum_k[...].astype(BF16)
    d_value[...] = sum_v[...].astype(BF16)
    for d in range(n):
        rows = pl.ds(pl.multiple_of(lax.rem(me - d + n, n) * own_phones, own_phones), own_phones)
        d_phone_k[rows] = phones[d][0]
        d_phone_v[rows] = phones[d][1]


def finish(n, own_phones, chosen, own_k, own_v, low, high, returned, phones):
    frames, width = own_k.shape
    column = lambda rows: pl.BlockSpec((rows, DH), lambda h: (0, h))
    pair = lambda rows: pl.BlockSpec((2, rows, DH), lambda h: (0, 0, h))
    edge = low.shape[1]
    shape = jax.ShapeDtypeStruct
    return pl.pallas_call(
        functools.partial(finish_kernel, n, own_phones),
        name="finish",
        grid=(width // DH,),
        out_shape=[shape((frames, width), BF16)] * 2
        + [shape((n * own_phones, width), BF16)] * 2,
        in_specs=[spec(SMEM)]
        + [column(frames)] * 2
        + [pair(edge)] * 2
        + [pair(BLK)] * (n - 1)
        + [pair(own_phones)] * n,
        out_specs=[column(frames)] * 2 + [column(n * own_phones)] * 2,
        scratch_shapes=[VMEM((frames, DH), F32)] * 2,
        cost_estimate=pl.CostEstimate(
            flops=0, bytes_accessed=16 * frames * width, transcendentals=0
        ),
    )(chosen, own_k, own_v, low, high, *returned, *phones)


def local(
    queries,
    key_vectors,
    value_vectors,
    cotangent,
    w_out,
    phoneme_keys,
    phoneme_values,
    phrase_blocks,
    phrase_count,
    alignment,
):
    query, key, value, own_cot = queries[0], key_vectors[0], value_vectors[0], cotangent[0]
    frames, width = query.shape
    half_model = own_cot.shape[1]
    phones = phoneme_keys.shape[1]
    n = lax.axis_size("ctx")
    dp = lax.axis_size("dp")
    me = lax.axis_index("ctx")
    side = lax.axis_index("head")
    own_phones = phones // n
    fixed = n - 1 <= PHRASE_SLOTS
    groups = n - 1 if fixed else PHRASE_SLOTS
    window = -(-(own_phones + 2 * PH_PAD) // BLK) * BLK

    first_rows, last_rows, sends, index = prepare(
        n, groups, fixed, phrase_blocks, phrase_count, key, value
    )
    chosen, place, bias = index
    low = shifted(last_rows, "ctx", 1)
    high = shifted(first_rows, "ctx", -1)
    received = [[rotated(s[d], "ctx", d + 1) for d in range(n - 1)] for s in sends]
    other_cot = swapped(own_cot, "head", 1)
    own_w = lax.dynamic_slice_in_dim(w_out, side * half_model, half_model, 1)
    other_w = lax.dynamic_slice_in_dim(w_out, (1 - side) * half_model, half_model, 1)
    partner_w = swapped(other_w, "head", 1)

    padded = [
        lax.dynamic_slice_in_dim(
            jnp.pad(p[0], ((PH_PAD, window - PH_PAD), (0, 0))), me * own_phones, window, 0
        )
        for p in (phoneme_keys, phoneme_values)
    ]
    grad = (mm(own_cot, own_w, NT) + mm(other_cot, other_w, NT)).astype(BF16)
    aligned = alignment[0][:, None]
    pieces = [
        attend(
            n,
            groups,
            fixed,
            own_phones,
            phones,
            c,
            (place, bias),
            aligned,
            query,
            grad,
            key,
            value,
            (low, high),
            padded,
            received[c],
        )
        for c in range(CHUNKS)
    ]
    joined = [
        pieces[0][k] if CHUNKS == 1 else jnp.concatenate([p[k] for p in pieces], axis=-1)
        for k in range(7)
    ]
    attended, d_query, own_k, own_v, to_prev, to_next, phone_own = joined
    from_next = shifted(to_prev, "ctx", -1)
    from_prev = shifted(to_next, "ctx", 1)
    returned = [
        [rotated(piece[7 + d], "ctx", -(d + 1)) for d in range(n - 1)] for piece in pieces
    ]
    returned = [
        returned[0][d]
        if CHUNKS == 1
        else jnp.concatenate([r[d] for r in returned], axis=-1)
        for d in range(n - 1)
    ]

    phone_sum = phone_own
    reach = -(-PH_PAD // own_phones)
    for k in range(1, reach + 1):
        lo = max(PH_PAD - own_phones * k, 0)
        hi = PH_PAD - own_phones * (k - 1)
        if k == 1:
            below = from_next[:, HALF_BAND + lo : HALF_BAND + hi]
            above = from_prev[:, HALF_BAND : HALF_BAND + hi - lo]
        else:
            below = shifted(to_prev[:, HALF_BAND + lo : HALF_BAND + hi], "ctx", -k)
            skip = own_phones * (k - 1)
            above = shifted(
                to_next[:, HALF_BAND + skip : HALF_BAND + skip + hi - lo], "ctx", k
            )
        at = own_phones * k - PH_PAD + lo
        tail = own_phones - at - (hi - lo)
        phone_sum = phone_sum + jnp.pad(below.astype(F32), ((0, 0), (at, tail), (0, 0)))
        tail = own_phones - (hi - lo)
        phone_sum = phone_sum + jnp.pad(above.astype(F32), ((0, 0), (0, tail), (0, 0)))
    phone_sum = phone_sum.astype(BF16)
    all_phones = [phone_sum] + [rotated(phone_sum, "ctx", d) for d in range(1, n)]
    d_key, d_value, d_phone_k, d_phone_v = finish(
        n, own_phones, chosen, own_k, own_v, from_prev, from_next, returned, all_phones
    )

    partner = swapped(attended, "head", 1)
    layer_out = (mm(attended, own_w, NN) + mm(partner, partner_w, NN)).astype(BF16)

    model = 2 * half_model
    columns = model // (n * dp)
    norm = 1.0 / math.sqrt(dp * n * frames)
    if columns % 128 == 0 and dp & (dp - 1) == 0:
        mine = lax.axis_index("dp")
        slot = jnp.arange(n * dp, dtype=jnp.int32)
        where = lax.rem(me + slot % n, n) * dp + (mine ^ (slot // n))
        per_half = half_model // columns
        terms = weight_terms(
            (where // per_half) ^ side, where % per_half, attended, own_cot, other_cot, columns
        )
        for bit in reversed(range(dp.bit_length() - 1)):
            half = terms.shape[0] // 2
            got = swapped(terms[half:], "dp", 1 << bit)
            terms = (terms[:half].astype(F32) + got.astype(F32)).astype(BF16)
        total = terms[0].astype(F32)
        for d in range(1, n):
            total = total + rotated(terms[d], "ctx", d).astype(F32)
        d_w_out = total * norm
    else:
        both = jnp.where(
            side == 0,
            jnp.concatenate([own_cot, other_cot], axis=1),
            jnp.concatenate([other_cot, own_cot], axis=1),
        )
        weight_term = mm(attended, both, TN)
        d_w_out = lax.psum_scatter(weight_term, ("ctx", "dp"), scatter_dimension=1, tiled=True)
        d_w_out = d_w_out * norm
    return (
        layer_out[None],
        d_query[None],
        d_key[None],
        d_value[None],
        d_phone_k[None],
        d_phone_v[None],
        d_w_out,
    )


def solution(mesh):
    placed = (
        P("dp", "ctx", "head"),
        P("dp", "ctx", "head"),
        P("dp", "ctx", "head"),
        P("dp", "ctx", "head"),
        P("head", None),
        P("dp", None, "head"),
        P("dp", None, "head"),
        P("dp", None, None),
        P("dp", "ctx"),
        P("dp", "ctx"),
    )
    return jax.shard_map(
        local,
        mesh=mesh,
        in_specs=placed,
        out_specs=(
            P("dp", "ctx", "head"),
            P("dp", "ctx", "head"),
            P("dp", "ctx", "head"),
            P("dp", "ctx", "head"),
            P("dp", None, "head"),
            P("dp", None, "head"),
            P("head", ("ctx", "dp")),
        ),
        check_vma=False,
    )
```
